32 devices in a mesh: pipe: 8 (over z, core), expert: 4 (over y, x).
Axes of the slice: x: 2, y: 2, z: 4, core: 2. Of those that a mesh axis runs over, the one named last changes fastest.
Arguments:
- acts: bfloat16 [8, 512, 3584], P('pipe', 'expert'), may hold values from -6 to 6
- routing: int32 [8, 512, 8], P('pipe', 'expert'), may hold values from 0 to 255, as said below
- combine_w: float32 [8, 512, 8], P('pipe', 'expert'), may hold values from 0.25 to 2.5
- w_gate_up: bfloat16 [8, 3584, 4096], P('pipe', None, 'expert'), may hold values from -0.09375 to 0.09375
- w_down: bfloat16 [8, 2048, 3584], P('pipe', 'expert'), may hold values from -0.125 to 0.125
Outputs:
- next_acts: bfloat16 [8, 512, 3584], P('pipe', 'expert')
The draws below stay inside these ranges and needn't reach their ends.
Inputs may be any that keep to these rules, and one draw needn't show every extreme that they name: `routing`: each row names 8 different experts. Within one section every aligned block of 128 rows (the rows of one device) holds the same number of rows naming expert 0, at least 1 and at most 8; in one section of every draw, drawn from the seed, exactly 8.
All inputs are finite; a program needn't handle non-finite values.
Results may differ from the reference program's by a relative error of at most 0.0055.
Values may be sent and summed in bfloat16 or wider, within the bound.
A program may use at most 64 MiB of HBM per device.

```python
import jax
import jax.numpy as jnp
from jax import lax

D = 3584
FF = 2048
ROUTED = 256
TOPK = 8
TOK_DEV = 128
CAP = 8
SECT = 8
TOKENS = 512
HID_DEV = 512
N_EXPERT = 4


def draw_routing(key, part):
    per_section = TOKENS // TOK_DEV
    blocks = per_section * SECT
    key_list = jax.random.split(key, 6)
    columns = jnp.arange(ROUTED)
    scores = jax.random.randint(key_list[1], (blocks, TOK_DEV, ROUTED), 0, 1 << 20) * ROUTED + columns
    scores = jnp.where(columns < 1, -1, scores)
    fillers = lax.top_k(scores, TOPK)[1].astype(jnp.int32)
    first_keys = jax.random.randint(key_list[2], (blocks, TOK_DEV), 0, 1 << 20) * TOK_DEV + jnp.arange(TOK_DEV)
    first_rank = jnp.argsort(jnp.argsort(first_keys, axis=1), axis=1)
    counts = jax.random.randint(key_list[3], (SECT, 1), 1, CAP + 1)
    full_section = jax.random.randint(key_list[0], (), 0, SECT)
    counts = jnp.where(jnp.arange(SECT)[:, None] == full_section, CAP, counts)
    block_counts = jnp.repeat(counts, per_section, axis=0)
    in_hot = first_rank < block_counts
    column_zero = jnp.where(in_hot, 0, fillers[..., 0])
    listed = jnp.concatenate([column_zero[..., None], fillers[..., 1:]], axis=-1)
    shuffle_keys = jax.random.randint(key_list[5], (blocks, TOK_DEV, TOPK), 0, 1 << 20) * TOPK + jnp.arange(TOPK)
    shuffle_order = jnp.argsort(shuffle_keys, axis=-1)
    listed = jnp.take_along_axis(listed, shuffle_order, axis=-1)
    return listed.reshape(SECT, TOKENS, TOPK).astype(jnp.int32)


def block_levels(own_key, extent, cuts, smallest, top_value):
    loudness, own = 1.0, jax.random.fold_in(own_key, 6)
    for dim, shards_of in cuts:
        steps = jnp.exp(jax.random.uniform(jax.random.fold_in(own, dim), (shards_of,), jnp.float32, smallest / len(cuts), top_value / len(cuts)))
        loudness = loudness * jnp.repeat(steps, extent[dim] // shards_of).reshape([-1 if axis == dim else 1 for axis in range(len(extent))])
    return loudness


def normal_values(key, dims, spread, most, cuts=(), held_as=jnp.bfloat16):
    level = block_levels(key, dims, cuts, -0.22, 0.18) if cuts else 1.0
    entries = jax.random.normal(key, dims, jnp.float32) * spread * level
    return jnp.minimum(jnp.maximum(entries, -most), most).astype(held_as)


def setup_inputs(seed: int = 0) -> dict:
    streams_of = jax.random.split(jax.random.key(seed), 6)
    return {
        "acts": normal_values(streams_of[0], (SECT, TOKENS, D), 1.0, 6.0, ((0, 8), (1, 4))),
        "routing": draw_routing(jax.random.fold_in(streams_of[5], 71), 0),
        "combine_w": jnp.clip(0.25 + 2.25 * jax.random.uniform(streams_of[2], (SECT, TOKENS, TOPK), jnp.float32) ** block_levels(streams_of[2], (SECT, TOKENS, TOPK), ((0, 8), (1, 4)), -0.2, 0.2), 0.25, 2.5),
        "w_gate_up": normal_values(streams_of[3], (SECT, D, 2 * FF), D ** -0.5, 0.09375, ((0, 8), (2, 4))),
        "w_down": normal_values(streams_of[4], (SECT, FF, D), FF ** -0.5, 0.125, ((0, 8), (1, 4))),
    }


def section_layer(tokens_in, route_ids, mix_weights, w_gate_up, w_down):
    row_count = N_EXPERT * CAP
    names_zero = route_ids == 0
    chosen = jnp.any(names_zero, axis=1)
    coefficient = jnp.sum(jnp.where(names_zero, mix_weights, 0.0), axis=1)
    picked = jnp.nonzero(chosen, size=row_count, fill_value=0)[0].astype(jnp.int32)
    valid_slot = jnp.arange(row_count, dtype=jnp.int32) < jnp.sum(chosen.astype(jnp.int32))
    rows_in = tokens_in[picked]
    paired = w_gate_up.reshape(D, N_EXPERT, 2, HID_DEV)
    gate_cols = paired[:, :, 0, :].reshape(D, FF)
    up_cols = paired[:, :, 1, :].reshape(D, FF)
    gate_part = jnp.dot(rows_in, gate_cols, preferred_element_type=jnp.float32)
    up_part = jnp.dot(rows_in, up_cols, preferred_element_type=jnp.float32)
    hidden = (jax.nn.silu(gate_part) * up_part).astype(jnp.bfloat16)
    blocks = hidden.astype(jnp.float32).reshape(row_count, N_EXPERT, HID_DEV)
    down_rows = w_down.astype(jnp.float32).reshape(N_EXPERT, HID_DEV, D)
    partial_value = jnp.einsum('ngh,ghd->ngd', blocks, down_rows).astype(jnp.bfloat16)
    merged = jnp.sum(partial_value.astype(jnp.float32), axis=1)
    scale_rows = jnp.where(valid_slot, coefficient[picked], 0.0)
    total_rows = jnp.zeros(tokens_in.shape, jnp.float32).at[picked].add(scale_rows[:, None] * merged)
    return (tokens_in.astype(jnp.float32) + total_rows).astype(jnp.bfloat16)


def reference(acts, routing, combine_w, w_gate_up, w_down):
    def one_section(section_items):
        return section_layer(*section_items)

    layers = lax.map(one_section, (acts, routing, combine_w, w_gate_up, w_down))
    return jnp.roll(layers, 1, axis=0)
```

```python
import functools

import jax
import jax.numpy as jnp
from jax import lax
from jax.experimental import pallas as pl
from jax.experimental.pallas import tpu as pltpu
from jax.sharding import PartitionSpec as P

CAP = 8
MESH = pl.DeviceIdType.MESH


def layer_rows(
    stages,
    peers,
    gather_pieces,
    load_pieces,
    part_pieces,
    acts,
    routing,
    combine_w,
    w_gate_up,
    w_down,
    rows_recv,
    acts_v,
    route_v,
    mix_v,
    gate_up_v,
    down_v,
    gathered,
    part_send,
    part_recv,
    rows_send,
    load_sem,
    gate_up_sem,
    down_sem,
    gather_send_sem,
    gather_recv_sem,
    part_send_sem,
    part_recv_sem,
    rows_sem,
):
    stage = lax.axis_index("pipe")
    me = lax.axis_index("expert")
    after = lax.rem(stage + 1, stages)
    before = lax.rem(stage + stages - 1, stages)
    width = acts.shape[2]
    tokens = acts.shape[1]
    hid = w_down.shape[1]
    gather_step = width // gather_pieces
    load_step = width // load_pieces
    part_step = width // part_pieces

    barrier = pltpu.get_barrier_semaphore()
    for k in range(1, peers):
        pl.semaphore_signal(
            barrier, inc=1, device_id=(stage, lax.rem(me + k, peers)), device_id_type=MESH
        )
    pl.semaphore_signal(barrier, inc=1, device_id=(before, me), device_id_type=MESH)
    pl.semaphore_signal(barrier, inc=1, device_id=(after, me), device_id_type=MESH)

    load_route = pltpu.make_async_copy(routing.at[0], route_v, load_sem.at[0])
    load_mix = pltpu.make_async_copy(combine_w.at[0], mix_v, load_sem.at[1])
    load_acts = pltpu.make_async_copy(acts.at[0], acts_v, load_sem.at[2])
    load_route.start()
    load_mix.start()
    load_acts.start()
    gate_up_loads = []
    for p in range(load_pieces):
        span = pl.ds(p * load_step, load_step)
        load = pltpu.make_async_copy(
            w_gate_up.at[0, span, :], gate_up_v.at[span, :], gate_up_sem.at[p]
        )
        load.start(priority=1)
        gate_up_loads.append(load)
    load_down = pltpu.make_async_copy(w_down.at[0], down_v, down_sem)
    load_down.start(priority=1)

    load_route.wait()
    load_mix.wait()
    named = route_v[...] == 0
    chosen = jnp.max(jnp.where(named, 1.0, 0.0), axis=0, keepdims=True)
    coefficient = jnp.sum(jnp.where(named, mix_v[...], 0.0), axis=0, keepdims=True)
    earlier = (
        lax.broadcasted_iota(jnp.int32, (tokens, tokens), 0)
        <= lax.broadcasted_iota(jnp.int32, (tokens, tokens), 1)
    ).astype(jnp.float32)
    count = jnp.dot(
        jnp.broadcast_to(chosen, (CAP, tokens)), earlier, preferred_element_type=jnp.float32
    )
    slot = lax.broadcasted_iota(jnp.int32, (CAP, tokens), 0).astype(jnp.float32) + 1.0
    select = jnp.where((count == slot) & (chosen > 0.5), 1.0, 0.0)
    slot_coeff = jnp.sum(select * coefficient, axis=1, keepdims=True)
    select_b = select.astype(jnp.bfloat16)
    rows_send[:, pl.ds(width, tokens)] = select_b

    load_acts.wait()
    for p in range(gather_pieces):
        cols = pl.ds(p * gather_step, gather_step)
        gathered[me, :, cols] = jnp.dot(
            select_b, acts_v[:, cols], preferred_element_type=jnp.float32
        ).astype(jnp.bfloat16)

    pl.semaphore_wait(barrier, peers + 1)

    def gather_copy(p, k, incoming):
        other = lax.rem(me + k, peers)
        source = other if incoming else me
        block = gathered.at[source, :, pl.ds(p * gather_step, gather_step)]
        return pltpu.make_async_remote_copy(
            src_ref=block,
            dst_ref=block,
            send_sem=gather_send_sem.at[p, k],
            recv_sem=gather_recv_sem.at[p, source],
            device_id=(stage, other),
            device_id_type=MESH,
        )

    for p in range(gather_pieces):
        for k in range(1, peers):
            gather_copy(p, k, False).start()

    total = None
    for p in range(load_pieces):
        span = pl.ds(p * load_step, load_step)
        if p % (load_pieces // gather_pieces) == 0:
            for k in range(1, peers):
                gather_copy(p * gather_pieces // load_pieces, k, True).wait_recv()
        rows = (
            gathered[:, :, span]
            .astype(jnp.float32)
            .reshape(peers * CAP, load_step)
            .astype(jnp.bfloat16)
        )
        gate_up_loads[p].wait()
        term = jnp.dot(rows, gate_up_v[span, :], preferred_element_type=jnp.float32)
        total = term if total is None else total + term
    gate = total[:, :hid]
    up = total[:, hid:]
    hidden = (gate / (1.0 + jnp.exp(-gate)) * up).astype(jnp.bfloat16)

    load_down.wait()

    def part_copy(p, k, source_side):
        other = lax.rem(me + k, peers)
        cols = pl.ds(p * part_step, part_step)
        return pltpu.make_async_remote_copy(
            src_ref=part_send.at[other, :, cols],
            dst_ref=part_recv.at[other if source_side else me, :, cols],
            send_sem=part_send_sem.at[p, k],
            recv_sem=part_recv_sem.at[p, other if source_side else me],
            device_id=(stage, other),
            device_id_type=MESH,
        )

    for p in range(part_pieces):
        cols = pl.ds(p * part_step, part_step)
        part = jnp.dot(hidden, down_v[:, cols], preferred_element_type=jnp.float32)
        part_send[:, :, cols] = part.reshape(peers, CAP, part_step).astype(jnp.bfloat16)
        for k in range(1, peers):
            part_copy(p, k, False).start()

    forwards = []
    for p in range(part_pieces):
        extra = tokens if p == part_pieces - 1 else 0
        cols = pl.ds(p * part_step, part_step + extra)
        forwards.append(
            pltpu.make_async_remote_copy(
                src_ref=rows_send.at[:, cols],
                dst_ref=rows_recv.at[:, cols],
                send_sem=rows_sem.at[0, p],
                recv_sem=rows_sem.at[1, p],
                device_id=(after, me),
                device_id_type=MESH,
            )
        )
    for p in range(part_pieces):
        cols = pl.ds(p * part_step, part_step)
        merged = part_send[me, :, cols].astype(jnp.float32)
        for k in range(1, peers):
            part_copy(p, k, True).wait_recv()
            merged = merged + part_recv[lax.rem(me + k, peers), :, cols].astype(jnp.float32)
        rows_send[:, cols] = (merged * slot_coeff).astype(jnp.bfloat16)
        forwards[p].start()
    for p in range(part_pieces):
        for k in range(1, peers):
            part_copy(p, k, False).wait_send()
    for p in range(gather_pieces):
        for k in range(1, peers):
            gather_copy(p, k, False).wait_send()
    for forward in forwards:
        forward.wait()


def add_rows(row_pieces, landed, rows, out, ready, sem):
    tokens, width = landed.shape[1:]
    step = tokens // row_pieces
    copies = []
    for p in range(row_pieces):
        span = pl.ds(p * step, step)
        layer = lax.dot_general(
            rows[:, pl.ds(width + p * step, step)],
            rows[:, pl.ds(0, width)],
            (((0,), (0,)), ((), ())),
            preferred_element_type=jnp.float32,
        )
        ready[0, span, :] = (landed[0, span, :].astype(jnp.float32) + layer).astype(ready.dtype)
        copy = pltpu.make_async_copy(ready.at[:, span, :], out.at[:, span, :], sem.at[p])
        copy.start()
        copies.append(copy)
    for copy in copies:
        copy.wait()


def per_device(stages, peers, acts, routing, combine_w, w_gate_up, w_down):
    _, tokens, width = acts.shape
    landed = lax.ppermute(acts, "pipe", [(i, (i + 1) % stages) for i in range(stages)])
    gather_pieces = 4
    load_pieces = 4
    part_pieces = 4
    row_pieces = 4
    anywhere = pl.BlockSpec(memory_space=pl.ANY)
    in_vmem = pl.BlockSpec(memory_space=pltpu.VMEM)
    dma = pltpu.SemaphoreType.DMA
    operands = (
        acts,
        jnp.swapaxes(routing, 1, 2),
        jnp.swapaxes(combine_w, 1, 2),
        w_gate_up,
        w_down,
    )
    rows = pl.pallas_call(
        functools.partial(layer_rows, stages, peers, gather_pieces, load_pieces, part_pieces),
        out_shape=pltpu.VMEM((CAP, width + tokens), jnp.bfloat16),
        in_specs=[anywhere] * 5,
        out_specs=in_vmem,
        scratch_shapes=[
            pltpu.VMEM((tokens, width), acts.dtype),
            pltpu.VMEM(operands[1].shape[1:], routing.dtype),
            pltpu.VMEM(operands[2].shape[1:], combine_w.dtype),
            pltpu.VMEM(w_gate_up.shape[1:], w_gate_up.dtype),
            pltpu.VMEM(w_down.shape[1:], w_down.dtype),
            pltpu.VMEM((peers, CAP, width), jnp.bfloat16),
            pltpu.VMEM((peers, CAP, width), jnp.bfloat16),
            pltpu.VMEM((peers, CAP, width), jnp.bfloat16),
            pltpu.VMEM((CAP, width + tokens), jnp.bfloat16),
            dma((3,)),
            dma((load_pieces,)),
            dma,
            dma((gather_pieces, peers)),
            dma((gather_pieces, peers)),
            dma((part_pieces, peers)),
            dma((part_pieces, peers)),
            dma((2, part_pieces)),
        ],
        compiler_params=pltpu.CompilerParams(
            collective_id=0, has_side_effects=True, vmem_limit_bytes=32 * 2**20
        ),
        cost_estimate=pl.CostEstimate(
            flops=6 * peers * CAP * width * w_down.shape[1],
            bytes_accessed=2 * (w_gate_up.size + w_down.size + acts.size),
            transcendentals=peers * CAP * w_down.shape[1],
        ),
        name="layer_rows",
    )(*(pltpu.with_memory_space_constraint(a, pltpu.HBM) for a in operands))
    return pl.pallas_call(
        functools.partial(add_rows, row_pieces),
        out_shape=jax.ShapeDtypeStruct(acts.shape, acts.dtype),
        in_specs=[in_vmem, in_vmem],
        out_specs=anywhere,
        scratch_shapes=[pltpu.VMEM(acts.shape, acts.dtype), dma((row_pieces,))],
        compiler_params=pltpu.CompilerParams(vmem_limit_bytes=8 * 2**20),
        name="add_rows",
    )(
        pltpu.with_memory_space_constraint(landed, pltpu.VMEM),
        pltpu.with_memory_space_constraint(rows, pltpu.VMEM),
    )


def solution(mesh):
    return jax.shard_map(
        functools.partial(per_device, mesh.shape["pipe"], mesh.shape["expert"]),
        mesh=mesh,
        in_specs=(
            P("pipe", "expert", None),
            P("pipe", "expert", None),
            P("pipe", "expert", None),
            P("pipe", None, "expert"),
            P("pipe", "expert", None),
        ),
        out_specs=P("pipe", "expert", None),
        check_vma=False,
    )
```

```python
import functools

import jax
import jax.numpy as jnp
from jax import lax
from jax.experimental import pallas as pl
from jax.experimental.pallas import tpu as pltpu
from jax.sharding import PartitionSpec as P

CAP = 8
MESH = pl.DeviceIdType.MESH


def relay_tick(
    stages,
    peers,
    gather_pieces,
    load_pieces,
    part_pieces,
    acts,
    routing,
    combine_w,
    w_gate_up,
    w_down,
    out,
    landed,
    acts_v,
    route_v,
    mix_v,
    gate_up_v,
    down_v,
    gathered,
    part_send,
    part_recv,
    rows_send,
    rows_recv,
    load_sem,
    gate_up_sem,
    down_sem,
    stream_sem,
    gather_send_sem,
    gather_recv_sem,
    part_send_sem,
    part_recv_sem,
    rows_sem,
    peers_in,
):
    stage = lax.axis_index("pipe")
    me = lax.axis_index("expert")
    after = lax.rem(stage + 1, stages)
    before = lax.rem(stage + stages - 1, stages)
    is_last = stage == stages - 1
    is_next_to_last = stage == stages - 2
    _, tokens, width = acts.shape
    hid = w_down.shape[1]
    gather_step = width // gather_pieces
    load_step = width // load_pieces
    part_step = width // part_pieces

    barrier = pltpu.get_barrier_semaphore()

    def say_in(where, who):
        pl.semaphore_signal(barrier, inc=1, device_id=(where, who), device_id_type=MESH)

    say_in_before = functools.partial(say_in, before)

    @pl.when(is_last)
    def _():
        for k in range(peers):
            say_in_before(lax.rem(me + k, peers))

    @pl.when(jnp.logical_not(is_last))
    def _():
        for k in range(1, peers):
            say_in(stage, lax.rem(me + k, peers))
        say_in_before(me)

    @pl.when(is_next_to_last)
    def _():
        pl.semaphore_wait(barrier, 2 * peers - 1)
        pl.semaphore_signal(peers_in, inc=1, device_id=(after, me), device_id_type=MESH)

    load_route = pltpu.make_async_copy(routing.at[0], route_v, load_sem.at[0])
    load_mix = pltpu.make_async_copy(combine_w.at[0], mix_v, load_sem.at[1])
    load_acts = pltpu.make_async_copy(acts.at[0], acts_v, load_sem.at[2])
    load_route.start()
    load_mix.start()
    load_acts.start()
    stream = pltpu.make_async_remote_copy(
        src_ref=acts.at[0],
        dst_ref=landed,
        send_sem=stream_sem.at[0],
        recv_sem=stream_sem.at[1],
        device_id=(after, me),
        device_id_type=MESH,
    )
    @pl.when(is_last)
    def _():
        pl.semaphore_wait(barrier, 1)
        stream.start()

    gate_up_loads = []
    for p in range(load_pieces):
        span = pl.ds(p * load_step, load_step)
        load = pltpu.make_async_copy(
            w_gate_up.at[0, span, :], gate_up_v.at[span, :], gate_up_sem.at[p]
        )
        load.start(priority=1)
        gate_up_loads.append(load)
    load_down = pltpu.make_async_copy(w_down.at[0], down_v, down_sem)
    load_down.start(priority=1)

    load_route.wait()
    load_mix.wait()
    named = route_v[...] == 0
    chosen = jnp.max(jnp.where(named, 1.0, 0.0), axis=0, keepdims=True)
    coefficient = jnp.sum(jnp.where(named, mix_v[...], 0.0), axis=0, keepdims=True)
    earlier = jnp.where(
        lax.broadcasted_iota(jnp.int32, (tokens, tokens), 0)
        <= lax.broadcasted_iota(jnp.int32, (tokens, tokens), 1),
        1.0,
        0.0,
    ).astype(jnp.bfloat16)
    count = jnp.dot(
        jnp.broadcast_to(chosen, (CAP, tokens)).astype(jnp.bfloat16),
        earlier,
        preferred_element_type=jnp.float32,
    )
    slot = lax.broadcasted_iota(jnp.int32, (CAP, tokens), 0).astype(jnp.float32) + 1.0
    select = jnp.where((count == slot) & (chosen > 0.5), 1.0, 0.0)
    slot_coeff = jnp.sum(select * coefficient, axis=1, keepdims=True)
    select_b = select.astype(jnp.bfloat16)
    rows_send[:, pl.ds(0, tokens)] = select_b

    def gather_copy(p, k, incoming):
        other = lax.rem(me + k, peers)
        source = other if incoming else me
        block = gathered.at[source, :, pl.ds(p * gather_step, gather_step)]
        return pltpu.make_async_remote_copy(
            src_ref=block,
            dst_ref=block,
            send_sem=gather_send_sem.at[p, k],
            recv_sem=gather_recv_sem.at[p, source],
            device_id=(stage, other),
            device_id_type=MESH,
        )

    load_acts.wait()
    for p in range(gather_pieces):
        cols = pl.ds(p * gather_step, gather_step)
        gathered[me, :, cols] = jnp.dot(
            select_b, acts_v[:, cols], preferred_element_type=jnp.float32
        ).astype(jnp.bfloat16)
        if p == 0:

            @pl.when(is_last)
            def _():
                pl.semaphore_wait(peers_in, 1)

            @pl.when(stage < stages - 2)
            def _():
                pl.semaphore_wait(barrier, peers)

        if p >= 0:
            for q in range(0 if p == 0 else p, p + 1):
                for k in range(1, peers):
                    gather_copy(q, k, False).start()

    @pl.when(jnp.logical_not(is_last))
    def _():
        stream.start()

    total = None
    for p in range(load_pieces):
        span = pl.ds(p * load_step, load_step)
        if p % (load_pieces // gather_pieces) == 0:
            for k in range(1, peers):
                gather_copy(p * gather_pieces // load_pieces, k, True).wait_recv()
        rows = (
            gathered[:, :, span]
            .astype(jnp.float32)
            .reshape(peers * CAP, load_step)
            .astype(jnp.bfloat16)
        )
        gate_up_loads[p].wait()
        term = jnp.dot(rows, gate_up_v[span, :], preferred_element_type=jnp.float32)
        total = term if total is None else total + term
    gate = total[:, :hid]
    up = total[:, hid:]
    hidden = (gate / (1.0 + jnp.exp(-gate)) * up).astype(jnp.bfloat16)

    def part_copy(p, k, incoming):
        other = lax.rem(me + k, peers)
        source = other if incoming else me
        cols = pl.ds(p * part_step, part_step)
        return pltpu.make_async_remote_copy(
            src_ref=part_send.at[other, :, cols],
            dst_ref=part_recv.at[source, :, cols],
            send_sem=part_send_sem.at[p, k],
            recv_sem=part_recv_sem.at[p, source],
            device_id=(stage, other),
            device_id_type=MESH,
        )

    load_down.wait()
    for p in range(part_pieces):
        cols = pl.ds(p * part_step, part_step)
        part = jnp.dot(hidden, down_v[:, cols], preferred_element_type=jnp.float32)
        part_send[:, :, cols] = part.reshape(peers, CAP, part_step).astype(jnp.bfloat16)
        for k in range(1, peers):
            part_copy(p, k, False).start()

    forwards = []
    for p in range(part_pieces):
        start = tokens + p * part_step if p else 0
        cols = pl.ds(start, tokens + (p + 1) * part_step - start)
        forwards.append(
            pltpu.make_async_remote_copy(
                src_ref=rows_send.at[:, cols],
                dst_ref=rows_recv.at[:, cols],
                send_sem=rows_sem.at[0, p],
                recv_sem=rows_sem.at[1, p],
                device_id=(after, me),
                device_id_type=MESH,
            )
        )
    for p in range(part_pieces):
        cols = pl.ds(p * part_step, part_step)
        merged = part_send[me, :, cols].astype(jnp.float32)
        for k in range(1, peers):
            part_copy(p, k, True).wait_recv()
            merged = merged + part_recv[lax.rem(me + k, peers), :, cols].astype(jnp.float32)
        rows_send[:, pl.ds(tokens + p * part_step, part_step)] = (merged * slot_coeff).astype(
            jnp.bfloat16
        )
        forwards[p].start()

    for p in range(gather_pieces):
        for k in range(1, peers):
            gather_copy(p, k, False).wait_send()
    for p in range(part_pieces):
        for k in range(1, peers):
            part_copy(p, k, False).wait_send()
    for p in range(part_pieces):
        forwards[p].wait_recv()
        if p == 0:
            place = rows_recv[:, pl.ds(0, tokens)]
            stream.wait_recv()
        cols = pl.ds(p * part_step, part_step)
        layer = lax.dot_general(
            place,
            rows_recv[:, pl.ds(tokens + p * part_step, part_step)],
            (((0,), (0,)), ((), ())),
            preferred_element_type=jnp.float32,
        )
        out[0, :, cols] = (landed[:, cols].astype(jnp.float32) + layer).astype(out.dtype)
    for forward in forwards:
        forward.wait_send()
    stream.wait_send()


def per_device(stages, peers, acts, routing, combine_w, w_gate_up, w_down):
    _, tokens, width = acts.shape
    gather_pieces = 4
    load_pieces = 4
    part_pieces = 4
    operands = (
        acts,
        jnp.swapaxes(routing, 1, 2),
        jnp.swapaxes(combine_w, 1, 2),
        w_gate_up,
        w_down,
    )
    dma = pltpu.SemaphoreType.DMA
    by_peer = pltpu.VMEM((peers, CAP, width), jnp.bfloat16)
    return pl.pallas_call(
        functools.partial(relay_tick, stages, peers, gather_pieces, load_pieces, part_pieces),
        out_shape=pltpu.VMEM(acts.shape, acts.dtype),
        in_specs=[pl.BlockSpec(memory_space=pl.ANY)] * 5,
        out_specs=pl.BlockSpec(memory_space=pltpu.VMEM),
        scratch_shapes=[
            pltpu.VMEM((tokens, width), acts.dtype),
            pltpu.VMEM((tokens, width), acts.dtype),
            pltpu.VMEM(operands[1].shape[1:], routing.dtype),
            pltpu.VMEM(operands[2].shape[1:], combine_w.dtype),
            pltpu.VMEM(w_gate_up.shape[1:], w_gate_up.dtype),
            pltpu.VMEM(w_down.shape[1:], w_down.dtype),
            by_peer,
            by_peer,
            by_peer,
            pltpu.VMEM((CAP, tokens + width), jnp.bfloat16),
            pltpu.VMEM((CAP, tokens + width), jnp.bfloat16),
            dma((3,)),
            dma((load_pieces,)),
            dma,
            dma((2,)),
            dma((gather_pieces, peers)),
            dma((gather_pieces, peers)),
            dma((part_pieces, peers)),
            dma((part_pieces, peers)),
            dma((2, part_pieces)),
            pltpu.SemaphoreType.REGULAR,
        ],
        compiler_params=pltpu.CompilerParams(
            collective_id=0, has_side_effects=True, vmem_limit_bytes=32 * 2**20
        ),
        name="relay_tick",
    )(*(pltpu.with_memory_space_constraint(a, pltpu.HBM) for a in operands))


def solution(mesh):
    return jax.shard_map(
        functools.partial(per_device, mesh.shape["pipe"], mesh.shape["expert"]),
        mesh=mesh,
        in_specs=(
            P("pipe", "expert", None),
            P("pipe", "expert", None),
            P("pipe", "expert", None),
            P("pipe", None, "expert"),
            P("pipe", "expert", None),
        ),
        out_specs=P("pipe", "expert", None),
        check_vma=False,
    )
```

```python
import functools

import jax
import jax.numpy as jnp
from jax import lax
from jax.experimental import pallas as pl
from jax.experimental.pallas import tpu as pltpu
from jax.sharding import PartitionSpec as P

CAP = 8
MESH = pl.DeviceIdType.MESH


def relay_tick(
    stages,
    peers,
    gather_pieces,
    load_pieces,
    part_pieces,
    acts,
    routing,
    combine_w,
    w_gate_up,
    w_down,
    out,
    landed,
    acts_v,
    route_v,
    mix_v,
    gate_up_v,
    down_v,
    gathered,
    part_send,
    part_recv,
    rows_send,
    rows_recv,
    load_sem,
    gate_up_sem,
    down_sem,
    stream_sem,
    gather_send_sem,
    gather_recv_sem,
    part_send_sem,
    part_recv_sem,
    rows_send_sem,
    rows_recv_sem,
    peers_in,
):
    stage = lax.axis_index("pipe")
    me = lax.axis_index("expert")
    after = lax.rem(stage + 1, stages)
    before = lax.rem(stage + stages - 1, stages)
    is_last = stage == stages - 1
    is_next_to_last = stage == stages - 2
    _, tokens, width = acts.shape
    hid = w_down.shape[1]
    gather_step = width // gather_pieces
    load_step = width // load_pieces
    part_step = width // part_pieces

    barrier = pltpu.get_barrier_semaphore()

    def say_in(where, who):
        pl.semaphore_signal(barrier, inc=1, device_id=(where, who), device_id_type=MESH)

    say_in_before = functools.partial(say_in, before)

    @pl.when(is_last)
    def _():
        for k in range(peers):
            say_in_before(lax.rem(me + k, peers))

    @pl.when(jnp.logical_not(is_last))
    def _():
        for k in range(1, peers):
            say_in(stage, lax.rem(me + k, peers))
        say_in_before(me)

    @pl.when(is_next_to_last)
    def _():
        pl.semaphore_wait(barrier, 2 * peers - 1)
        pl.semaphore_signal(peers_in, inc=1, device_id=(after, me), device_id_type=MESH)

    load_route = pltpu.make_async_copy(routing.at[0], route_v, load_sem.at[0])
    load_mix = pltpu.make_async_copy(combine_w.at[0], mix_v, load_sem.at[1])
    load_acts = pltpu.make_async_copy(acts.at[0], acts_v, load_sem.at[2])
    load_route.start()
    load_mix.start()
    load_acts.start()
    stream = pltpu.make_async_remote_copy(
        src_ref=acts.at[0],
        dst_ref=landed,
        send_sem=stream_sem.at[0],
        recv_sem=stream_sem.at[1],
        device_id=(after, me),
        device_id_type=MESH,
    )
    @pl.when(is_last)
    def _():
        pl.semaphore_wait(barrier, 1)
        stream.start()

    gate_up_loads = []
    for p in range(load_pieces):
        span = pl.ds(p * load_step, load_step)
        load = pltpu.make_async_copy(
            w_gate_up.at[0, span, :], gate_up_v.at[span, :], gate_up_sem.at[p]
        )
        load.start(priority=1)
        gate_up_loads.append(load)
    load_down = pltpu.make_async_copy(w_down.at[0], down_v, down_sem)
    load_down.start(priority=1)

    load_route.wait()
    load_mix.wait()
    named = route_v[...] == 0
    chosen = jnp.max(jnp.where(named, 1.0, 0.0), axis=0, keepdims=True)
    coefficient = jnp.sum(jnp.where(named, mix_v[...], 0.0), axis=0, keepdims=True)
    earlier = jnp.where(
        lax.broadcasted_iota(jnp.int32, (tokens, tokens), 0)
        <= lax.broadcasted_iota(jnp.int32, (tokens, tokens), 1),
        1.0,
        0.0,
    ).astype(jnp.bfloat16)
    count = jnp.dot(
        jnp.broadcast_to(chosen, (CAP, tokens)).astype(jnp.bfloat16),
        earlier,
        preferred_element_type=jnp.float32,
    )
    slot = lax.broadcasted_iota(jnp.int32, (CAP, tokens), 0).astype(jnp.float32) + 1.0
    select = jnp.where((count == slot) & (chosen > 0.5), 1.0, 0.0)
    slot_coeff = jnp.sum(select * coefficient, axis=1, keepdims=True)
    select_b = select.astype(jnp.bfloat16)
    rows_send[:, pl.ds(0, tokens)] = select_b

    def wait_all(ref, sem):
        pltpu.make_async_copy(ref, ref, sem).wait()

    def gather_copy(p, k):
        other = lax.rem(me + k, peers)
        block = gathered.at[me, :, pl.ds(p * gather_step, gather_step)]
        return pltpu.make_async_remote_copy(
            src_ref=block,
            dst_ref=block,
            send_sem=gather_send_sem,
            recv_sem=gather_recv_sem.at[p],
            device_id=(stage, other),
            device_id_type=MESH,
        )

    load_acts.wait()
    for p in range(gather_pieces):
        cols = pl.ds(p * gather_step, gather_step)
        gathered[me, :, cols] = jnp.dot(
            select_b, acts_v[:, cols], preferred_element_type=jnp.float32
        ).astype(jnp.bfloat16)
        if p == 0:

            @pl.when(is_last)
            def _():
                pl.semaphore_wait(peers_in, 1)

            @pl.when(stage < stages - 2)
            def _():
                pl.semaphore_wait(barrier, peers)

        if p >= 0:
            for q in range(0 if p == 0 else p, p + 1):
                for k in range(1, peers):
                    gather_copy(q, k).start()

    @pl.when(jnp.logical_not(is_last))
    def _():
        stream.start()

    total = None
    for p in range(load_pieces):
        span = pl.ds(p * load_step, load_step)
        if p % (load_pieces // gather_pieces) == 0:
            q = p * gather_pieces // load_pieces
            cols = pl.ds(q * gather_step, gather_step)
            wait_all(gathered.at[pl.ds(0, peers - 1), :, cols], gather_recv_sem.at[q])
        rows = (
            gathered[:, :, span]
            .astype(jnp.float32)
            .reshape(peers * CAP, load_step)
            .astype(jnp.bfloat16)
        )
        gate_up_loads[p].wait()
        term = jnp.dot(rows, gate_up_v[span, :], preferred_element_type=jnp.float32)
        total = term if total is None else total + term
    gate = total[:, :hid]
    up = total[:, hid:]
    hidden = (gate / (1.0 + jnp.exp(-gate)) * up).astype(jnp.bfloat16)

    def part_copy(p, k):
        other = lax.rem(me + k, peers)
        cols = pl.ds(p * part_step, part_step)
        return pltpu.make_async_remote_copy(
            src_ref=part_send.at[other, :, cols],
            dst_ref=part_recv.at[me, :, cols],
            send_sem=part_send_sem,
            recv_sem=part_recv_sem.at[p],
            device_id=(stage, other),
            device_id_type=MESH,
        )

    load_down.wait()
    for p in range(part_pieces):
        cols = pl.ds(p * part_step, part_step)
        part = jnp.dot(hidden, down_v[:, cols], preferred_element_type=jnp.float32)
        part_send[:, :, cols] = part.reshape(peers, CAP, part_step).astype(jnp.bfloat16)
        for k in range(1, peers):
            part_copy(p, k).start()

    forwards = []
    for p in range(part_pieces):
        start = tokens + p * part_step if p else 0
        cols = pl.ds(start, tokens + (p + 1) * part_step - start)
        forwards.append(
            pltpu.make_async_remote_copy(
                src_ref=rows_send.at[:, cols],
                dst_ref=rows_recv.at[:, cols],
                send_sem=rows_send_sem,
                recv_sem=rows_recv_sem.at[p],
                device_id=(after, me),
                device_id_type=MESH,
            )
        )
    for p in range(part_pieces):
        cols = pl.ds(p * part_step, part_step)
        wait_all(part_recv.at[pl.ds(0, peers - 1), :, cols], part_recv_sem.at[p])
        merged = part_send[me, :, cols].astype(jnp.float32)
        for k in range(1, peers):
            merged = merged + part_recv[lax.rem(me + k, peers), :, cols].astype(jnp.float32)
        rows_send[:, pl.ds(tokens + p * part_step, part_step)] = (merged * slot_coeff).astype(
            jnp.bfloat16
        )
        forwards[p].start()

    for p in range(part_pieces):
        forwards[p].wait_recv()
        if p == 0:
            place = rows_recv[:, pl.ds(0, tokens)]
            stream.wait_recv()
        cols = pl.ds(p * part_step, part_step)
        layer = lax.dot_general(
            place,
            rows_recv[:, pl.ds(tokens + p * part_step, part_step)],
            (((0,), (0,)), ((), ())),
            preferred_element_type=jnp.float32,
        )
        out[0, :, cols] = (landed[:, cols].astype(jnp.float32) + layer).astype(out.dtype)
    wait_all(gathered.at[pl.ds(0, peers - 1)], gather_send_sem)
    wait_all(part_send.at[pl.ds(0, peers - 1)], part_send_sem)
    wait_all(rows_send, rows_send_sem)
    stream.wait_send()


def per_device(stages, peers, acts, routing, combine_w, w_gate_up, w_down):
    _, tokens, width = acts.shape
    gather_pieces = 4
    load_pieces = 4
    part_pieces = 4
    operands = (
        acts,
        jnp.swapaxes(routing, 1, 2),
        jnp.swapaxes(combine_w, 1, 2),
        w_gate_up,
        w_down,
    )
    dma = pltpu.SemaphoreType.DMA
    by_peer = pltpu.VMEM((peers, CAP, width), jnp.bfloat16)
    return pl.pallas_call(
        functools.partial(relay_tick, stages, peers, gather_pieces, load_pieces, part_pieces),
        out_shape=pltpu.VMEM(acts.shape, acts.dtype),
        in_specs=[pl.BlockSpec(memory_space=pl.ANY)] * 5,
        out_specs=pl.BlockSpec(memory_space=pltpu.VMEM),
        scratch_shapes=[
            pltpu.VMEM((tokens, width), acts.dtype),
            pltpu.VMEM((tokens, width), acts.dtype),
            pltpu.VMEM(operands[1].shape[1:], routing.dtype),
            pltpu.VMEM(operands[2].shape[1:], combine_w.dtype),
            pltpu.VMEM(w_gate_up.shape[1:], w_gate_up.dtype),
            pltpu.VMEM(w_down.shape[1:], w_down.dtype),
            by_peer,
            by_peer,
            by_peer,
            pltpu.VMEM((CAP, tokens + width), jnp.bfloat16),
            pltpu.VMEM((CAP, tokens + width), jnp.bfloat16),
            dma((3,)),
            dma((load_pieces,)),
            dma,
            dma((2,)),
            dma,
            dma((gather_pieces,)),
            dma,
            dma((part_pieces,)),
            dma,
            dma((part_pieces,)),
            pltpu.SemaphoreType.REGULAR,
        ],
        compiler_params=pltpu.CompilerParams(
            collective_id=0, has_side_effects=True, vmem_limit_bytes=32 * 2**20
        ),
        name="relay_tick",
    )(*(pltpu.with_memory_space_constraint(a, pltpu.HBM) for a in operands))


def solution(mesh):
    return jax.shard_map(
        functools.partial(per_device, mesh.shape["pipe"], mesh.shape["expert"]),
        mesh=mesh,
        in_specs=(
            P("pipe", "expert", None),
            P("pipe", "expert", None),
            P("pipe", "expert", None),
            P("pipe", None, "expert"),
            P("pipe", "expert", None),
        ),
        out_specs=P("pipe", "expert", None),
        check_vma=False,
    )
```

```python
import functools

import jax
import jax.numpy as jnp
from jax import lax
from jax.experimental import pallas as pl
from jax.experimental.pallas import tpu as pltpu
from jax.sharding import PartitionSpec as P

CAP = 8
MESH = pl.DeviceIdType.MESH


def relay_tick(
    stages,
    peers,
    gather_pieces,
    load_pieces,
    part_pieces,
    acts,
    routing,
    combine_w,
    w_gate_up,
    w_down,
    out,
    landed,
    acts_v,
    route_v,
    mix_v,
    gate_up_v,
    down_v,
    gathered,
    part_send,
    part_recv,
    rows_send,
    rows_recv,
    load_sem,
    gate_up_sem,
    down_sem,
    stream_sem,
    gather_send_sem,
    gather_recv_sem,
    part_send_sem,
    part_recv_sem,
    rows_send_sem,
    rows_recv_sem,
    peers_in,
):
    stage = lax.axis_index("pipe")
    me = lax.axis_index("expert")
    after = lax.rem(stage + 1, stages)
    before = lax.rem(stage + stages - 1, stages)
    is_last = stage == stages - 1
    is_next_to_last = stage == stages - 2
    _, tokens, width = acts.shape
    hid = w_down.shape[1]
    gather_step = width // gather_pieces
    load_step = width // load_pieces
    part_step = width // part_pieces

    barrier = pltpu.get_barrier_semaphore()

    def say_in(where, who):
        pl.semaphore_signal(barrier, inc=1, device_id=(where, who), device_id_type=MESH)

    stream = pltpu.make_async_remote_copy(
        src_ref=acts.at[0],
        dst_ref=landed,
        send_sem=stream_sem.at[0],
        recv_sem=stream_sem.at[1],
        device_id=(after, me),
        device_id_type=MESH,
    )

    @pl.when(is_last & (me == 0))
    def _():
        pl.semaphore_wait(barrier, 1)
        stream.start()

    say_in_before = functools.partial(say_in, before)

    @pl.when(is_last)
    def _():
        for k in range(peers):
            say_in_before(lax.rem(me + k, peers))

    @pl.when(jnp.logical_not(is_last))
    def _():
        for k in range(1, peers):
            say_in(stage, lax.rem(me + k, peers))
        say_in_before(me)

    @pl.when(is_next_to_last)
    def _():
        pl.semaphore_wait(barrier, 2 * peers - 1)
        pl.semaphore_signal(peers_in, inc=1, device_id=(after, me), device_id_type=MESH)

    load_route = pltpu.make_async_copy(routing.at[0], route_v, load_sem.at[0])
    load_mix = pltpu.make_async_copy(combine_w.at[0], mix_v, load_sem.at[1])
    load_acts = pltpu.make_async_copy(acts.at[0], acts_v, load_sem.at[2])
    load_route.start()
    load_mix.start()
    load_acts.start()
    @pl.when(is_last & (me > 0))
    def _():
        pl.semaphore_wait(barrier, 1)
        stream.start()

    gate_up_loads = []
    for p in range(load_pieces):
        span = pl.ds(p * load_step, load_step)
        load = pltpu.make_async_copy(
            w_gate_up.at[0, span, :], gate_up_v.at[span, :], gate_up_sem.at[p]
        )
        load.start(priority=1)
        gate_up_loads.append(load)
    load_down = pltpu.make_async_copy(w_down.at[0], down_v, down_sem)
    load_down.start(priority=1)

    load_route.wait()
    load_mix.wait()
    named = route_v[...] == 0
    chosen = jnp.max(jnp.where(named, 1.0, 0.0), axis=0, keepdims=True)
    coefficient = jnp.sum(jnp.where(named, mix_v[...], 0.0), axis=0, keepdims=True)
    earlier = jnp.where(
        lax.broadcasted_iota(jnp.int32, (tokens, tokens), 0)
        <= lax.broadcasted_iota(jnp.int32, (tokens, tokens), 1),
        1.0,
        0.0,
    ).astype(jnp.bfloat16)
    count = jnp.dot(
        jnp.broadcast_to(chosen, (CAP, tokens)).astype(jnp.bfloat16),
        earlier,
        preferred_element_type=jnp.float32,
    )
    slot = lax.broadcasted_iota(jnp.int32, (CAP, tokens), 0).astype(jnp.float32) + 1.0
    select = jnp.where((count == slot) & (chosen > 0.5), 1.0, 0.0)
    slot_coeff = jnp.sum(select * coefficient, axis=1, keepdims=True)
    select_b = select.astype(jnp.bfloat16)
    rows_send[:, pl.ds(0, tokens)] = select_b

    def wait_all(ref, sem):
        pltpu.make_async_copy(ref, ref, sem).wait()

    def gather_copy(p, k):
        other = lax.rem(me + k, peers)
        block = gathered.at[me, :, pl.ds(p * gather_step, gather_step)]
        return pltpu.make_async_remote_copy(
            src_ref=block,
            dst_ref=block,
            send_sem=gather_send_sem,
            recv_sem=gather_recv_sem.at[p],
            device_id=(stage, other),
            device_id_type=MESH,
        )

    load_acts.wait()
    for p in range(gather_pieces):
        cols = pl.ds(p * gather_step, gather_step)
        gathered[me, :, cols] = jnp.dot(
            select_b, acts_v[:, cols], preferred_element_type=jnp.float32
        ).astype(jnp.bfloat16)
        if p == 3:

            @pl.when(is_last)
            def _():
                pl.semaphore_wait(peers_in, 1)

            @pl.when(stage < stages - 2)
            def _():
                pl.semaphore_wait(barrier, peers)

        if p >= 3:
            for q in range(0 if p == 3 else p, p + 1):
                for k in range(1, peers):
                    gather_copy(q, k).start()

    @pl.when(jnp.logical_not(is_last))
    def _():
        stream.start()

    total = None
    for p in range(load_pieces):
        span = pl.ds(p * load_step, load_step)
        if p % (load_pieces // gather_pieces) == 0:
            q = p * gather_pieces // load_pieces
            cols = pl.ds(q * gather_step, gather_step)
            wait_all(gathered.at[pl.ds(0, peers - 1), :, cols], gather_recv_sem.at[q])
        rows = (
            gathered[:, :, span]
            .astype(jnp.float32)
            .reshape(peers * CAP, load_step)
            .astype(jnp.bfloat16)
        )
        gate_up_loads[p].wait()
        term = jnp.dot(rows, gate_up_v[span, :], preferred_element_type=jnp.float32)
        total = term if total is None else total + term
    gate = total[:, :hid]
    up = total[:, hid:]
    hidden = (gate / (1.0 + jnp.exp(-gate)) * up).astype(jnp.bfloat16)

    def part_copy(p, k):
        other = lax.rem(me + k, peers)
        cols = pl.ds(p * part_step, part_step)
        return pltpu.make_async_remote_copy(
            src_ref=part_send.at[other, :, cols],
            dst_ref=part_recv.at[me, :, cols],
            send_sem=part_send_sem,
            recv_sem=part_recv_sem.at[p],
            device_id=(stage, other),
            device_id_type=MESH,
        )

    load_down.wait()
    for p in range(part_pieces):
        cols = pl.ds(p * part_step, part_step)
        part = jnp.dot(hidden, down_v[:, cols], preferred_element_type=jnp.float32)
        part_send[:, :, cols] = part.reshape(peers, CAP, part_step).astype(jnp.bfloat16)
        for k in range(1, peers):
            part_copy(p, k).start()

    forwards = []
    for p in range(part_pieces):
        start = tokens + p * part_step if p else 0
        cols = pl.ds(start, tokens + (p + 1) * part_step - start)
        forwards.append(
            pltpu.make_async_remote_copy(
                src_ref=rows_send.at[:, cols],
                dst_ref=rows_recv.at[:, cols],
                send_sem=rows_send_sem,
                recv_sem=rows_recv_sem.at[p],
                device_id=(after, me),
                device_id_type=MESH,
            )
        )
    for p in range(part_pieces):
        cols = pl.ds(p * part_step, part_step)
        wait_all(part_recv.at[pl.ds(0, peers - 1), :, cols], part_recv_sem.at[p])
        merged = part_send[me, :, cols].astype(jnp.float32)
        for k in range(1, peers):
            merged = merged + part_recv[lax.rem(me + k, peers), :, cols].astype(jnp.float32)
        rows_send[:, pl.ds(tokens + p * part_step, part_step)] = (merged * slot_coeff).astype(
            jnp.bfloat16
        )
        forwards[p].start()

    for p in range(part_pieces):
        forwards[p].wait_recv()
        if p == 0:
            place = rows_recv[:, pl.ds(0, tokens)]
            stream.wait_recv()
        cols = pl.ds(p * part_step, part_step)
        layer = lax.dot_general(
            place,
            rows_recv[:, pl.ds(tokens + p * part_step, part_step)],
            (((0,), (0,)), ((), ())),
            preferred_element_type=jnp.float32,
        )
        out[0, :, cols] = (landed[:, cols].astype(jnp.float32) + layer).astype(out.dtype)
    wait_all(gathered.at[pl.ds(0, peers - 1)], gather_send_sem)
    wait_all(part_send.at[pl.ds(0, peers - 1)], part_send_sem)
    wait_all(rows_send, rows_send_sem)
    stream.wait_send()


def per_device(stages, peers, acts, routing, combine_w, w_gate_up, w_down):
    _, tokens, width = acts.shape
    gather_pieces = 4
    load_pieces = 4
    part_pieces = 4
    operands = (
        acts,
        jnp.swapaxes(routing, 1, 2),
        jnp.swapaxes(combine_w, 1, 2),
        w_gate_up,
        w_down,
    )
    dma = pltpu.SemaphoreType.DMA
    by_peer = pltpu.VMEM((peers, CAP, width), jnp.bfloat16)
    return pl.pallas_call(
        functools.partial(relay_tick, stages, peers, gather_pieces, load_pieces, part_pieces),
        out_shape=pltpu.VMEM(acts.shape, acts.dtype),
        in_specs=[pl.BlockSpec(memory_space=pl.ANY)] * 5,
        out_specs=pl.BlockSpec(memory_space=pltpu.VMEM),
        scratch_shapes=[
            pltpu.VMEM((tokens, width), acts.dtype),
            pltpu.VMEM((tokens, width), acts.dtype),
            pltpu.VMEM(operands[1].shape[1:], routing.dtype),
            pltpu.VMEM(operands[2].shape[1:], combine_w.dtype),
            pltpu.VMEM(w_gate_up.shape[1:], w_gate_up.dtype),
            pltpu.VMEM(w_down.shape[1:], w_down.dtype),
            by_peer,
            by_peer,
            by_peer,
            pltpu.VMEM((CAP, tokens + width), jnp.bfloat16),
            pltpu.VMEM((CAP, tokens + width), jnp.bfloat16),
            dma((3,)),
            dma((load_pieces,)),
            dma,
            dma((2,)),
            dma,
            dma((gather_pieces,)),
            dma,
            dma((part_pieces,)),
            dma,
            dma((part_pieces,)),
            pltpu.SemaphoreType.REGULAR,
        ],
        compiler_params=pltpu.CompilerParams(
            collective_id=0, has_side_effects=True, vmem_limit_bytes=32 * 2**20
        ),
        name="relay_tick",
    )(*(pltpu.with_memory_space_constraint(a, pltpu.HBM) for a in operands))


def solution(mesh):
    return jax.shard_map(
        functools.partial(per_device, mesh.shape["pipe"], mesh.shape["expert"]),
        mesh=mesh,
        in_specs=(
            P("pipe", "expert", None),
            P("pipe", "expert", None),
            P("pipe", "expert", None),
            P("pipe", None, "expert"),
            P("pipe", "expert", None),
        ),
        out_specs=P("pipe", "expert", None),
        check_vma=False,
    )
```

```python
import functools

import jax
import jax.numpy as jnp
from jax import lax
from jax.experimental import pallas as pl
from jax.experimental.pallas import tpu as pltpu
from jax.sharding import PartitionSpec as P

CAP = 8
MESH = pl.DeviceIdType.MESH


def layer_rows(
    stages,
    peers,
    gather_pieces,
    load_pieces,
    part_pieces,
    acts,
    routing,
    combine_w,
    w_gate_up,
    w_down,
    rows_recv,
    acts_v,
    route_v,
    mix_v,
    gate_up_v,
    down_v,
    gathered,
    part_send,
    part_recv,
    rows_send,
    load_sem,
    gate_up_sem,
    down_sem,
    gather_send_sem,
    gather_recv_sem,
    part_send_sem,
    part_recv_sem,
    rows_send_sem,
    rows_recv_sem,
):
    stage = lax.axis_index("pipe")
    me = lax.axis_index("expert")
    after = lax.rem(stage + 1, stages)
    before = lax.rem(stage + stages - 1, stages)
    _, tokens, width = acts.shape
    hid = w_down.shape[1]
    gather_step = width // gather_pieces
    load_step = width // load_pieces
    part_step = width // part_pieces

    barrier = pltpu.get_barrier_semaphore()
    for k in range(1, peers):
        pl.semaphore_signal(
            barrier, inc=1, device_id=(stage, lax.rem(me + k, peers)), device_id_type=MESH
        )
    pl.semaphore_signal(barrier, inc=1, device_id=(before, me), device_id_type=MESH)
    pl.semaphore_signal(barrier, inc=1, device_id=(after, me), device_id_type=MESH)

    load_route = pltpu.make_async_copy(routing.at[0], route_v, load_sem.at[0])
    load_mix = pltpu.make_async_copy(combine_w.at[0], mix_v, load_sem.at[1])
    load_acts = pltpu.make_async_copy(acts.at[0], acts_v, load_sem.at[2])
    load_route.start()
    load_mix.start()
    load_acts.start()
    gate_up_loads = []
    for p in range(load_pieces):
        span = pl.ds(p * load_step, load_step)
        load = pltpu.make_async_copy(
            w_gate_up.at[0, span, :], gate_up_v.at[span, :], gate_up_sem.at[p]
        )
        load.start(priority=1)
        gate_up_loads.append(load)
    load_down = pltpu.make_async_copy(w_down.at[0], down_v, down_sem)
    load_down.start(priority=1)

    load_route.wait()
    load_mix.wait()
    named = route_v[...] == 0
    chosen = jnp.max(jnp.where(named, 1.0, 0.0), axis=0, keepdims=True)
    coefficient = jnp.sum(jnp.where(named, mix_v[...], 0.0), axis=0, keepdims=True)
    earlier = jnp.where(
        lax.broadcasted_iota(jnp.int32, (tokens, tokens), 0)
        <= lax.broadcasted_iota(jnp.int32, (tokens, tokens), 1),
        1.0,
        0.0,
    ).astype(jnp.bfloat16)
    count = jnp.dot(
        jnp.broadcast_to(chosen, (CAP, tokens)).astype(jnp.bfloat16),
        earlier,
        preferred_element_type=jnp.float32,
    )
    slot = lax.broadcasted_iota(jnp.int32, (CAP, tokens), 0).astype(jnp.float32) + 1.0
    select = jnp.where((count == slot) & (chosen > 0.5), 1.0, 0.0)
    slot_coeff = jnp.sum(select * coefficient, axis=1, keepdims=True)
    select_b = select.astype(jnp.bfloat16)
    rows_send[:, pl.ds(0, tokens)] = select_b

    def wait_all(ref, sem):
        pltpu.make_async_copy(ref, ref, sem).wait()

    def gather_copy(p, k, incoming):
        other = lax.rem(me + k, peers)
        source = other if incoming else me
        block = gathered.at[source, :, pl.ds(p * gather_step, gather_step)]
        return pltpu.make_async_remote_copy(
            src_ref=block,
            dst_ref=block,
            send_sem=gather_send_sem,
            recv_sem=gather_recv_sem.at[p],
            device_id=(stage, other),
            device_id_type=MESH,
        )

    load_acts.wait()
    for p in range(gather_pieces):
        cols = pl.ds(p * gather_step, gather_step)
        gathered[me, :, cols] = jnp.dot(
            select_b, acts_v[:, cols], preferred_element_type=jnp.float32
        ).astype(jnp.bfloat16)
        if p == 0:
            pl.semaphore_wait(barrier, peers + 1)
        if p >= 0:
            for q in range(0 if p == 0 else p, p + 1):
                for k in range(1, peers):
                    gather_copy(q, k, False).start()

    total = None
    for p in range(load_pieces):
        span = pl.ds(p * load_step, load_step)
        if p % (load_pieces // gather_pieces) == 0:
            q = p * gather_pieces // load_pieces
            cols = pl.ds(q * gather_step, gather_step)
            wait_all(gathered.at[pl.ds(0, peers - 1), :, cols], gather_recv_sem.at[q])
        rows = (
            gathered[:, :, span]
            .astype(jnp.float32)
            .reshape(peers * CAP, load_step)
            .astype(jnp.bfloat16)
        )
        gate_up_loads[p].wait()
        term = jnp.dot(rows, gate_up_v[span, :], preferred_element_type=jnp.float32)
        total = term if total is None else total + term
    gate = total[:, :hid]
    up = total[:, hid:]
    hidden = (gate / (1.0 + jnp.exp(-gate)) * up).astype(jnp.bfloat16)

    def part_copy(p, k, incoming):
        other = lax.rem(me + k, peers)
        source = other if incoming else me
        cols = pl.ds(p * part_step, part_step)
        return pltpu.make_async_remote_copy(
            src_ref=part_send.at[other, :, cols],
            dst_ref=part_recv.at[source, :, cols],
            send_sem=part_send_sem,
            recv_sem=part_recv_sem.at[p],
            device_id=(stage, other),
            device_id_type=MESH,
        )

    load_down.wait()
    for p in range(part_pieces):
        cols = pl.ds(p * part_step, part_step)
        part = jnp.dot(hidden, down_v[:, cols], preferred_element_type=jnp.float32)
        part_send[:, :, cols] = part.reshape(peers, CAP, part_step).astype(jnp.bfloat16)
        for k in range(1, peers):
            part_copy(p, k, False).start()

    forwards = []
    for p in range(part_pieces):
        start = tokens + p * part_step if p else 0
        cols = pl.ds(start, tokens + (p + 1) * part_step - start)
        forwards.append(
            pltpu.make_async_remote_copy(
                src_ref=rows_send.at[:, cols],
                dst_ref=rows_recv.at[:, cols],
                send_sem=rows_send_sem,
                recv_sem=rows_recv_sem.at[p],
                device_id=(after, me),
                device_id_type=MESH,
            )
        )
    for p in range(part_pieces):
        cols = pl.ds(p * part_step, part_step)
        wait_all(part_recv.at[pl.ds(0, peers - 1), :, cols], part_recv_sem.at[p])
        merged = part_send[me, :, cols].astype(jnp.float32)
        for k in range(1, peers):
            merged = merged + part_recv[lax.rem(me + k, peers), :, cols].astype(jnp.float32)
        rows_send[:, pl.ds(tokens + p * part_step, part_step)] = (merged * slot_coeff).astype(
            jnp.bfloat16
        )
        forwards[p].start()

    wait_all(gathered.at[pl.ds(0, peers - 1)], gather_send_sem)
    wait_all(part_send.at[pl.ds(0, peers - 1)], part_send_sem)
    wait_all(rows_send, rows_send_sem)
    for forward in forwards:
        forward.wait_recv()


def add_rows(row_pieces, landed, rows, out, ready, sem):
    tokens, width = landed.shape[1:]
    step = width // row_pieces
    copies = []
    for p in range(row_pieces):
        span = pl.ds(p * step, step)
        layer = lax.dot_general(
            rows[:, pl.ds(0, tokens)],
            rows[:, pl.ds(tokens + p * step, step)],
            (((0,), (0,)), ((), ())),
            preferred_element_type=jnp.float32,
        )
        ready[0, :, span] = (landed[0, :, span].astype(jnp.float32) + layer).astype(ready.dtype)
        copy = pltpu.make_async_copy(ready.at[:, :, span], out.at[:, :, span], sem.at[p])
        copy.start()
        copies.append(copy)
    for copy in copies:
        copy.wait()


def per_device(stages, peers, acts, routing, combine_w, w_gate_up, w_down):
    _, tokens, width = acts.shape
    landed = lax.ppermute(acts, "pipe", [(i, (i + 1) % stages) for i in range(stages)])
    gather_pieces = 4
    load_pieces = 4
    part_pieces = 4
    row_pieces = 7
    operands = (
        acts,
        jnp.swapaxes(routing, 1, 2),
        jnp.swapaxes(combine_w, 1, 2),
        w_gate_up,
        w_down,
    )
    dma = pltpu.SemaphoreType.DMA
    by_peer = pltpu.VMEM((peers, CAP, width), jnp.bfloat16)
    rows = pl.pallas_call(
        functools.partial(layer_rows, stages, peers, gather_pieces, load_pieces, part_pieces),
        out_shape=pltpu.VMEM((CAP, tokens + width), jnp.bfloat16),
        in_specs=[pl.BlockSpec(memory_space=pl.ANY)] * 5,
        out_specs=pl.BlockSpec(memory_space=pltpu.VMEM),
        scratch_shapes=[
            pltpu.VMEM((tokens, width), acts.dtype),
            pltpu.VMEM(operands[1].shape[1:], routing.dtype),
            pltpu.VMEM(operands[2].shape[1:], combine_w.dtype),
            pltpu.VMEM(w_gate_up.shape[1:], w_gate_up.dtype),
            pltpu.VMEM(w_down.shape[1:], w_down.dtype),
            by_peer,
            by_peer,
            by_peer,
            pltpu.VMEM((CAP, tokens + width), jnp.bfloat16),
            dma((3,)),
            dma((load_pieces,)),
            dma,
            dma,
            dma((gather_pieces,)),
            dma,
            dma((part_pieces,)),
            dma,
            dma((part_pieces,)),
        ],
        compiler_params=pltpu.CompilerParams(
            collective_id=0, has_side_effects=True, vmem_limit_bytes=32 * 2**20
        ),
        cost_estimate=pl.CostEstimate(
            flops=6 * peers * CAP * width * w_down.shape[1],
            bytes_accessed=2 * (w_gate_up.size + w_down.size + acts.size),
            transcendentals=peers * CAP * w_down.shape[1],
        ),
        name="layer_rows",
    )(*(pltpu.with_memory_space_constraint(a, pltpu.HBM) for a in operands))
    return pl.pallas_call(
        functools.partial(add_rows, row_pieces),
        out_shape=jax.ShapeDtypeStruct(acts.shape, acts.dtype),
        in_specs=[pl.BlockSpec(memory_space=pltpu.VMEM)] * 2,
        out_specs=pl.BlockSpec(memory_space=pl.ANY),
        scratch_shapes=[pltpu.VMEM(acts.shape, acts.dtype), dma((row_pieces,))],
        compiler_params=pltpu.CompilerParams(vmem_limit_bytes=8 * 2**20),
        name="add_rows",
    )(
        pltpu.with_memory_space_constraint(landed, pltpu.VMEM),
        pltpu.with_memory_space_constraint(rows, pltpu.VMEM),
    )


def solution(mesh):
    return jax.shard_map(
        functools.partial(per_device, mesh.shape["pipe"], mesh.shape["expert"]),
        mesh=mesh,
        in_specs=(
            P("pipe", "expert", None),
            P("pipe", "expert", None),
            P("pipe", "expert", None),
            P("pipe", None, "expert"),
            P("pipe", "expert", None),
        ),
        out_specs=P("pipe", "expert", None),
        check_vma=False,
    )
```
